1024 devices in a mesh: ctx: 32 (over y, x), head: 32 (over z, core).
Axes of the slice: x: 4, y: 8, z: 16, core: 2. Of those that a mesh axis runs over, the one named last changes fastest.
Arguments:
- query_rows: bfloat16 [49152, 4096], P(('ctx', 'head')), may hold values from -6 to 6
- key_rows: bfloat16 [49152, 4096], P(('ctx', 'head')), may hold values from -6 to 6
- value_rows: bfloat16 [49152, 4096], P('ctx', 'head'), may hold values from -6 to 6
- out_grad: bfloat16 [49152, 4096], P('ctx', 'head'), may hold values from -6 to 6
- entry_state: float32 [32, 128, 128], P('head'), may hold values from -1330.215 to 1330.215
Outputs:
- attended: bfloat16 [49152, 4096], P(('ctx', 'head'))
- query_grad: bfloat16 [49152, 4096], P('ctx', 'head')
- key_grad: bfloat16 [49152, 4096], P('ctx', 'head')
- value_grad: bfloat16 [49152, 4096], P('ctx', 'head')
- state_grad: float32 [32, 128, 128], P('head')
The draws below stay inside these ranges and needn't reach their ends.
All inputs are finite; a program needn't handle non-finite values.
Results may differ from the reference program's by a relative error of at most 0.0049.
Values may be sent and summed in bfloat16 or wider, within the bound.
A program may use at most 32 MiB of HBM per device.

```python
import jax
import jax.numpy as jnp
from jax import lax

HEADS = 32
HEAD_DIM = 128
SPAN = 384
TOKENS = 49152
FEATURES = 4096


def levels(key, extent, cuts, least, largest):
    gain = 1.0
    for position, shards_of in cuts:
        draws = jax.random.uniform(jax.random.fold_in(jax.random.fold_in(key, 6), position), (shards_of,), jnp.float32, least / len(cuts), largest / len(cuts))
        gain = gain * jnp.repeat(jnp.exp(draws), extent[position] // shards_of).reshape((-1,) + (1,) * (len(extent) - 1 - position))
    return gain


def bell_draw(stream_key, extent, deviation, most, cuts=(), dtype=jnp.bfloat16):
    array = deviation * jax.random.normal(stream_key, extent, jnp.float32)
    if cuts:
        array = array * levels(stream_key, extent, cuts, -0.22, 0.18)
    return jnp.clip(array, -most, most).astype(dtype)


def setup_inputs(seed: int = 0) -> dict:
    arg_keys = jax.random.split(jax.random.key(seed), 6)
    return {
        "query_rows": bell_draw(arg_keys[0], (TOKENS, FEATURES), 1.0, 6.0, ((0, 1024),)),
        "key_rows": bell_draw(arg_keys[1], (TOKENS, FEATURES), 1.0, 6.0, ((0, 1024),)),
        "value_rows": bell_draw(arg_keys[2], (TOKENS, FEATURES), 1.0, 6.0, ((0, 32), (1, 32))),
        "out_grad": bell_draw(arg_keys[3], (TOKENS, FEATURES), 1.0, 6.0, ((0, 32), (1, 32))),
        "entry_state": bell_draw(arg_keys[4], (HEADS, HEAD_DIM, HEAD_DIM), (TOKENS ** 0.5), 1330.215, ((0, 32),), jnp.float32),
    }


def reference(query_rows, key_rows, value_rows, out_grad, entry_state):
    scale = 1.0 / (HEAD_DIM * TOKENS) ** 0.5
    blocks = TOKENS // SPAN
    shape4 = (blocks, SPAN, HEADS, HEAD_DIM)
    query_all = query_rows.reshape(shape4)
    key_all = key_rows.reshape(shape4)
    value_all = value_rows.reshape(shape4)
    grad_all = out_grad.reshape(shape4)
    rows = jnp.arange(SPAN)
    causal = rows[:, None] >= rows[None, :]

    def forward_step(state, pieces):
        query_b, key_b, value_b, grad_b = [p.astype(jnp.float32) for p in pieces]
        state_low = state.astype(jnp.bfloat16).astype(jnp.float32)
        scores = jnp.where(causal[None], jnp.einsum('chd,shd->hcs', query_b, key_b), 0.0).astype(jnp.bfloat16).astype(jnp.float32)
        errors = jnp.where(causal[None], jnp.einsum('che,she->hcs', grad_b, value_b), 0.0).astype(jnp.bfloat16).astype(jnp.float32)
        attended = scale * (jnp.einsum('chd,hde->che', query_b, state_low) + jnp.einsum('hcs,she->che', scores, value_b))
        query_grad = scale * (jnp.einsum('che,hde->chd', grad_b, state_low) + jnp.einsum('hcs,shd->chd', errors, key_b))
        state_next = state + jnp.einsum('chd,che->hde', key_b, value_b)
        return state_next, (attended.astype(jnp.bfloat16), query_grad.astype(jnp.bfloat16))

    _, (attended, query_grad) = lax.scan(forward_step, entry_state.astype(jnp.float32), (query_all, key_all, value_all, grad_all))

    def backward_step(adjoint, pieces):
        query_b, key_b, value_b, grad_b = [p.astype(jnp.float32) for p in pieces]
        adjoint_low = adjoint.astype(jnp.bfloat16).astype(jnp.float32)
        scores = jnp.where(causal[None], jnp.einsum('chd,shd->hcs', query_b, key_b), 0.0).astype(jnp.bfloat16).astype(jnp.float32)
        errors = jnp.where(causal[None], jnp.einsum('che,she->hcs', grad_b, value_b), 0.0).astype(jnp.bfloat16).astype(jnp.float32)
        key_grad = scale * (jnp.einsum('che,hde->chd', value_b, adjoint_low) + jnp.einsum('hcs,chd->shd', errors, query_b))
        value_grad = scale * (jnp.einsum('chd,hde->che', key_b, adjoint_low) + jnp.einsum('hcs,che->she', scores, grad_b))
        adjoint_next = adjoint + jnp.einsum('chd,che->hde', query_b, grad_b)
        return adjoint_next, (key_grad.astype(jnp.bfloat16), value_grad.astype(jnp.bfloat16))

    zero_state = jnp.zeros((HEADS, HEAD_DIM, HEAD_DIM), jnp.float32)
    total, (key_grad, value_grad) = lax.scan(backward_step, zero_state, (query_all, key_all, value_all, grad_all), reverse=True)
    flat = (TOKENS, HEADS * HEAD_DIM)
    return (attended.reshape(flat), query_grad.reshape(flat), key_grad.reshape(flat), value_grad.reshape(flat), scale * total)
```

```python
import functools
import math

import jax
import jax.numpy as jnp
from jax import lax
from jax.experimental import pallas as pl
from jax.experimental.pallas import tpu as pltpu
from jax.sharding import PartitionSpec as P

SPAN = 384
XS = 4
MESH = pl.DeviceIdType.MESH
F32 = jnp.float32
BF16 = jnp.bfloat16


def dot(a, b, ca, cb):
    return lax.dot_general(a, b, (((ca,), (cb,)), ((), ())), preferred_element_type=F32)


def kernel(
    cfg,
    q_hbm, k_hbm, v_hbm, g_hbm, s_hbm,
    att_out, qgrad_out, kgrad_out, vgrad_out, sgrad_out,
    k_send, q_send, k_all, q_all, v_all, g_all, s_own,
    att_send, att_recv,
    errors, scores, kv_blk, qg_blk, qgrad_part, kgrad_part, vgrad_part,
    own_quarter, row_in, row_sum, col_in, back_out, back_in,
    load_sem, send_sem, k_sem, q_sem, att_sem,
    ex_send, ex_recv,
):
    zs, ys, rows, dim, blocks, scale = cfg
    heads = 2 * zs
    per_block = SPAN // rows
    ctx = lax.axis_index("ctx")
    me = lax.axis_index("head")
    z = lax.div(me, 2)
    core = lax.rem(me, 2)
    y = lax.div(ctx, XS)
    x = lax.rem(ctx, XS)
    my_block = lax.div(me, per_block)
    my_rows = pl.ds(pl.multiple_of(me * rows, rows), rows)

    def columns(h):
        return pl.ds(pl.multiple_of(h * dim, dim), dim)

    def block_rows(b):
        return pl.ds(pl.multiple_of(b * SPAN, SPAN), SPAN)

    for src, dst, sem in ((k_hbm, k_send, 0), (q_hbm, q_send, 1)):
        @pl.loop(0, heads)
        def _(h):
            pltpu.make_async_copy(src.at[:, columns(h)], dst.at[h], load_sem.at[sem]).start()
    pltpu.make_async_copy(k_hbm.at[:, columns(me)], k_all.at[my_rows], k_sem.at[my_block]).start()
    pltpu.make_async_copy(q_hbm.at[:, columns(me)], q_all.at[my_rows], q_sem.at[my_block]).start()
    load_v = pltpu.make_async_copy(v_hbm, v_all, load_sem.at[2])
    load_g = pltpu.make_async_copy(g_hbm, g_all, load_sem.at[3])
    load_s = pltpu.make_async_copy(s_hbm, s_own, load_sem.at[4])
    load_v.start()
    load_g.start()
    load_s.start()

    barrier = pltpu.get_barrier_semaphore()

    @pl.loop(1, heads)
    def _(i):
        pl.semaphore_signal(
            barrier, inc=1, device_id={"head": lax.rem(me + i, heads)}, device_id_type=MESH
        )

    @pl.loop(1, XS)
    def _(i):
        pl.semaphore_signal(
            barrier, inc=1, device_id={"ctx": y * XS + lax.rem(x + i, XS)}, device_id_type=MESH
        )

    @pl.loop(1, ys)
    def _(i):
        pl.semaphore_signal(
            barrier, inc=1, device_id={"ctx": lax.rem(y + i, ys) * XS + x}, device_id_type=MESH
        )

    pltpu.make_async_copy(k_send, k_send, load_sem.at[0]).wait()
    pltpu.make_async_copy(q_send, q_send, load_sem.at[1]).wait()
    load_v.wait()
    load_g.wait()
    load_s.wait()
    pl.semaphore_wait(barrier, heads - 1 + XS - 1 + ys - 1)

    def post(src, dst, sem, recv, peer):
        pltpu.make_async_remote_copy(
            src_ref=src.at[peer], dst_ref=dst.at[my_rows], send_sem=send_sem.at[sem],
            recv_sem=recv.at[my_block], device_id={"head": peer}, device_id_type=MESH,
        ).start()

    for src, dst, sem, recv in ((k_send, k_all, 0, k_sem), (q_send, q_all, 1, q_sem)):
        post(src, dst, sem, recv, 2 * z + 1 - core)

        @pl.loop(1, zs)
        def _(i):
            step = lax.div(i + 1, 2) * (2 * lax.rem(i, 2) - 1)
            peer_z = lax.rem(z + step + zs, zs)
            post(src, dst, sem, recv, 2 * peer_z + core)
            post(src, dst, sem, recv, 2 * peer_z + 1 - core)

    causal = lax.broadcasted_iota(jnp.int32, (SPAN, SPAN), 0) >= lax.broadcasted_iota(
        jnp.int32, (SPAN, SPAN), 1
    )

    @pl.loop(0, blocks)
    def _(b):
        at = block_rows(b)
        errors[b] = jnp.where(causal, dot(g_all[at], v_all[at], 1, 1), 0.0).astype(BF16)

    for b in range(blocks):
        pltpu.make_async_copy(
            k_all.at[pl.ds(b * SPAN, SPAN)], k_all.at[pl.ds(b * SPAN, SPAN)], k_sem.at[b]
        ).wait()

    quarter = dim // XS

    def send_x(which, src_of, dst, i):
        to = lax.rem(x + i, XS)
        pltpu.make_async_remote_copy(
            src_ref=src_of(to), dst_ref=dst, send_sem=ex_send.at[which],
            recv_sem=ex_recv.at[which], device_id={"ctx": y * XS + to}, device_id_type=MESH,
        ).start()

    def stage_quarters(n, total):
        own_quarter[n] = total.reshape(XS, quarter, dim)
        for i in range(1, XS):
            send_x(3 * n, lambda to: own_quarter.at[n, to], row_in.at[n, x], i)
        row_in[n, x] = own_quarter[n, x]

    def stage_rows(n):
        three = row_in.at[n, pl.ds(0, XS - 1)]
        pltpu.make_async_copy(three, three, ex_recv.at[3 * n]).wait()
        total = row_in[n, 0]
        for i in range(1, XS):
            total = total + row_in[n, i]
        row_sum[n] = total
        for i in range(1, ys):
            pltpu.make_async_remote_copy(
                src_ref=row_sum.at[n], dst_ref=col_in.at[n, y], send_sem=ex_send.at[3 * n + 1],
                recv_sem=ex_recv.at[3 * n + 1],
                device_id={"ctx": lax.rem(y + i, ys) * XS + x}, device_id_type=MESH,
            ).start()
        col_in[n, y] = total

    def stage_back(n):
        rest = col_in.at[n, pl.ds(0, ys - 1)]
        pltpu.make_async_copy(rest, rest, ex_recv.at[3 * n + 1]).wait()
        zero = jnp.zeros((quarter, dim), F32)
        part = zero
        for i in range(ys):
            keep = (i > y) if n else (i < y)
            part = part + jnp.where(keep, col_in[n, i], zero)
        if n:
            grand = col_in[n, 0]
            for i in range(1, ys):
                grand = grand + col_in[n, i]
        members = range(XS - 1, -1, -1) if n else range(XS)
        for m in members:
            back_out[n, m, 0] = part
            if n:
                back_out[n, m, 1] = grand
            part = part + row_in[n, m]
        planes = 2 if n else 1
        for i in range(1, XS):
            send_x(
                3 * n + 2, lambda to: back_out.at[n, to, pl.ds(0, planes)],
                back_in.at[n, x, pl.ds(0, planes)], i,
            )
        back_in[n, x, 0] = back_out[n, x, 0]
        if n:
            back_in[n, x, 1] = back_out[n, x, 1]

    def stage_done(n):
        planes = 2 if n else 1
        three = back_in.at[n, pl.ds(0, XS - 1), pl.ds(0, planes)]
        pltpu.make_async_copy(three, three, ex_recv.at[3 * n + 2]).wait()

    total = jnp.zeros((dim, dim), F32)
    for b in range(blocks):
        at = pl.ds(b * SPAN, SPAN)
        kv_blk[b] = total
        total = total + dot(k_all[at], v_all[at], 0, 0)
    stage_quarters(0, total)

    def inner_query_grad(b):
        at = block_rows(b)
        qgrad_part[at] = dot(errors[b], k_all[at], 1, 0)

    inner_query_grad(0)
    inner_query_grad(1)
    stage_rows(0)
    inner_query_grad(2)
    inner_query_grad(3)
    stage_back(0)
    stage_done(0)
    state_in = s_own[0] + back_in[0, :, 0].reshape(dim, dim)
    for b in range(blocks):
        kv_blk[b] = kv_blk[b] + state_in

    def attend(b):
        at = block_rows(b)
        pltpu.make_async_copy(q_all.at[at], q_all.at[at], q_sem.at[b]).wait()
        q_b = q_all[at]
        low = jnp.where(causal, dot(q_b, k_all[at], 1, 1), 0.0).astype(BF16)
        scores[b] = low
        out = dot(q_b, kv_blk[b].astype(BF16), 1, 0) + dot(low, v_all[at], 1, 0)
        att_send[at] = (scale * out).astype(BF16)

    def give_back(owner):
        pltpu.make_async_remote_copy(
            src_ref=att_send.at[pl.ds(pl.multiple_of(owner * rows, rows), rows)],
            dst_ref=att_recv.at[me], send_sem=send_sem.at[2], recv_sem=att_sem,
            device_id={"head": owner}, device_id_type=MESH,
        ).start()

    def state_of_queries(b):
        at = block_rows(b)
        qg_blk[b] = dot(q_all[at], g_all[at], 0, 0)

    attend(my_block)
    place = lax.rem(me, per_block)

    @pl.loop(1, per_block)
    def _(j):
        give_back(my_block * per_block + lax.rem(place + j, per_block))

    pltpu.make_async_copy(att_send.at[my_rows], att_recv.at[me], att_sem).start()
    state_of_queries(my_block)

    low_side = lax.div(place, per_block // 2)

    @pl.loop(1, blocks)
    def _(i):
        step = jnp.where(i == 1, 2 * low_side - 1, jnp.where(i == 2, 1 - 2 * low_side, 2))
        b = lax.rem(my_block + step + blocks, blocks)
        attend(b)

        @pl.loop(0, per_block)
        def _(j):
            give_back(b * per_block + j)

        state_of_queries(b)

    total = jnp.zeros((dim, dim), F32)
    for b in range(blocks - 1, -1, -1):
        own = qg_blk[b]
        qg_blk[b] = total
        total = total + own
    stage_quarters(1, total)

    def inner_grads(b):
        at = block_rows(b)
        kgrad_part[at] = dot(errors[b], q_all[at], 0, 0)
        vgrad_part[at] = dot(scores[b], g_all[at], 0, 0)

    def query_grad(b):
        at = block_rows(b)
        out = dot(g_all[at], kv_blk[b].astype(BF16), 1, 1) + qgrad_part[at]
        qgrad_out[at] = (scale * out).astype(BF16)

    inner_grads(0)
    inner_grads(1)
    stage_rows(1)
    inner_grads(2)
    inner_grads(3)
    for b in range(blocks):
        query_grad(b)
    stage_back(1)
    stage_done(1)
    after = back_in[1, :, 0].reshape(dim, dim)
    sgrad_out[0] = scale * back_in[1, :, 1].reshape(dim, dim)
    for b in range(blocks):
        at = pl.ds(b * SPAN, SPAN)
        low = (after + qg_blk[b]).astype(BF16)
        kgrad_out[at] = (scale * (dot(v_all[at], low, 1, 1) + kgrad_part[at])).astype(BF16)
        vgrad_out[at] = (scale * (dot(k_all[at], low, 1, 0) + vgrad_part[at])).astype(BF16)

    pltpu.make_async_copy(att_recv, att_recv, att_sem).wait()
    for h in range(heads):
        att_out[:, h * dim : (h + 1) * dim] = att_recv[h]

    others = pl.ds(0, heads - 1)
    pltpu.make_async_copy(k_send.at[others], k_send.at[others], send_sem.at[0]).wait()
    pltpu.make_async_copy(q_send.at[others], q_send.at[others], send_sem.at[1]).wait()
    pltpu.make_async_copy(att_recv.at[others], att_recv.at[others], send_sem.at[2]).wait()
    for n in range(2):
        three = row_in.at[n, pl.ds(0, XS - 1)]
        pltpu.make_async_copy(three, three, ex_send.at[3 * n]).wait()
        rest = col_in.at[n, pl.ds(0, ys - 1)]
        pltpu.make_async_copy(rest, rest, ex_send.at[3 * n + 1]).wait()
        three = back_in.at[n, pl.ds(0, XS - 1), pl.ds(0, 2 if n else 1)]
        pltpu.make_async_copy(three, three, ex_send.at[3 * n + 2]).wait()


def local(zs, ys, query_rows, key_rows, value_rows, out_grad, entry_state):
    rows, features = query_rows.shape
    length, dim = value_rows.shape
    heads = 2 * zs
    blocks = length // SPAN
    scale = 1.0 / math.sqrt(dim * length * ys * XS)
    quarter = dim // XS
    any_spec = pl.BlockSpec(memory_space=pl.ANY)
    vmem_spec = pl.BlockSpec(memory_space=pltpu.VMEM)
    dma = pltpu.SemaphoreType.DMA
    wide = (length, dim)
    return pl.pallas_call(
        functools.partial(kernel, (zs, ys, rows, dim, blocks, scale)),
        out_shape=(
            jax.ShapeDtypeStruct((rows, features), BF16),
            jax.ShapeDtypeStruct(wide, BF16),
            jax.ShapeDtypeStruct(wide, BF16),
            jax.ShapeDtypeStruct(wide, BF16),
            jax.ShapeDtypeStruct((1, dim, dim), F32),
        ),
        in_specs=[any_spec] * 5,
        out_specs=[vmem_spec] * 5,
        scratch_shapes=[
            pltpu.VMEM((heads, rows, dim), BF16),
            pltpu.VMEM((heads, rows, dim), BF16),
            pltpu.VMEM(wide, BF16),
            pltpu.VMEM(wide, BF16),
            pltpu.VMEM(wide, BF16),
            pltpu.VMEM(wide, BF16),
            pltpu.VMEM((1, dim, dim), F32),
            pltpu.VMEM(wide, BF16),
            pltpu.VMEM((heads, rows, dim), BF16),
            pltpu.VMEM((blocks, SPAN, SPAN), BF16),
            pltpu.VMEM((blocks, SPAN, SPAN), BF16),
            pltpu.VMEM((blocks, dim, dim), F32),
            pltpu.VMEM((blocks, dim, dim), F32),
            pltpu.VMEM(wide, F32),
            pltpu.VMEM(wide, F32),
            pltpu.VMEM(wide, F32),
            pltpu.VMEM((2, XS, quarter, dim), F32),
            pltpu.VMEM((2, XS, quarter, dim), F32),
            pltpu.VMEM((2, quarter, dim), F32),
            pltpu.VMEM((2, ys, quarter, dim), F32),
            pltpu.VMEM((2, XS, 2, quarter, dim), F32),
            pltpu.VMEM((2, XS, 2, quarter, dim), F32),
            dma((5,)),
            dma((3,)),
            dma((blocks,)),
            dma((blocks,)),
            dma,
            dma((6,)),
            dma((6,)),
        ],
        compiler_params=pltpu.CompilerParams(
            collective_id=0, has_side_effects=True, vmem_limit_bytes=40 * 1024 * 1024
        ),
        name="layer",
    )(query_rows, key_rows, value_rows, out_grad, entry_state)


def solution(mesh):
    ys = mesh.shape["ctx"] // XS
    zs = mesh.shape["head"] // 2
    tokens = P(("ctx", "head"), None)
    split = P("ctx", "head")
    state = P("head", None, None)
    return jax.shard_map(
        functools.partial(local, zs, ys),
        mesh=mesh,
        in_specs=(tokens, tokens, split, split, state),
        out_specs=(tokens, split, split, split, state),
        check_vma=False,
    )
```

```python
import functools
import math

import jax
import jax.numpy as jnp
from jax import lax
from jax.experimental import pallas as pl
from jax.experimental.pallas import tpu as pltpu
from jax.sharding import PartitionSpec as P

SPAN = 384
XS = 4
FAR_X = (2, 1, 3)
MESH = pl.DeviceIdType.MESH
F32 = jnp.float32
BF16 = jnp.bfloat16


def dot(a, b, ca, cb):
    return lax.dot_general(a, b, (((ca,), (cb,)), ((), ())), preferred_element_type=F32)


def kernel(
    cfg,
    q_hbm, k_hbm, v_hbm, g_hbm, s_hbm,
    att_out, qgrad_out, kgrad_out, vgrad_out, sgrad_out,
    k_send, q_send, k_all, q_all, v_all, g_all, s_own,
    att_send, att_recv,
    errors, scores, kv_blk, qg_blk, qgrad_part, kgrad_part, vgrad_part,
    own_quarter, row_in, row_sum, col_in, back_out, back_in,
    load_sem, send_sem, k_sem, q_sem, att_sem,
    ex_send, ex_recv,
):
    zs, ys, rows, dim, blocks, scale = cfg
    heads = 2 * zs
    per_block = SPAN // rows
    ctx = lax.axis_index("ctx")
    me = lax.axis_index("head")
    z = lax.div(me, 2)
    core = lax.rem(me, 2)
    y = lax.div(ctx, XS)
    x = lax.rem(ctx, XS)
    my_block = lax.div(me, per_block)
    my_rows = pl.ds(pl.multiple_of(me * rows, rows), rows)

    def columns(h):
        return pl.ds(pl.multiple_of(h * dim, dim), dim)

    def block_rows(b):
        return pl.ds(pl.multiple_of(b * SPAN, SPAN), SPAN)

    barrier = pltpu.get_barrier_semaphore()

    def greet(where):
        pl.semaphore_signal(barrier, inc=1, device_id=where, device_id_type=MESH)

    def chip_at(i):
        step = lax.div(i + 1, 2) * (2 * lax.rem(i, 2) - 1)
        return lax.rem(z + step + zs, zs)

    @pl.loop(1, zs)
    def _(i):
        far = chip_at(zs - i)
        greet({"head": 2 * far})
        greet({"head": 2 * far + 1})

    greet({"head": 2 * z + 1 - core})

    @pl.loop(1, XS)
    def _(i):
        greet({"ctx": y * XS + lax.rem(x + i, XS)})

    @pl.loop(1, ys)
    def _(i):
        greet({"ctx": lax.rem(y + i, ys) * XS + x})

    def load_pieces(src, dst, sem):
        @pl.loop(0, heads)
        def _(h):
            pltpu.make_async_copy(src.at[:, columns(h)], dst.at[h], load_sem.at[sem]).start()

    load_v = pltpu.make_async_copy(v_hbm, v_all, load_sem.at[2])
    load_g = pltpu.make_async_copy(g_hbm, g_all, load_sem.at[3])
    load_s = pltpu.make_async_copy(s_hbm, s_own, load_sem.at[4])
    with jax.named_scope("loads"):
        load_v.start()
        load_g.start()
        load_pieces(k_hbm, k_send, 0)
        pltpu.make_async_copy(k_hbm.at[:, columns(me)], k_all.at[my_rows], k_sem.at[my_block]).start()
        load_pieces(q_hbm, q_send, 1)
        pltpu.make_async_copy(q_hbm.at[:, columns(me)], q_all.at[my_rows], q_sem.at[my_block]).start()
        load_s.start()

    causal = lax.broadcasted_iota(jnp.int32, (SPAN, SPAN), 0) >= lax.broadcasted_iota(
        jnp.int32, (SPAN, SPAN), 1
    )

    with jax.named_scope("loadwait"):
        pltpu.make_async_copy(k_send, k_send, load_sem.at[0]).wait()
        pltpu.make_async_copy(q_send, q_send, load_sem.at[1]).wait()
    with jax.named_scope("barrier"):
        pl.semaphore_wait(barrier, heads - 1 + XS - 1 + ys - 1)

    def post(src, dst, sem, recv, peer):
        pltpu.make_async_remote_copy(
            src_ref=src.at[peer], dst_ref=dst.at[my_rows], send_sem=send_sem.at[sem],
            recv_sem=recv.at[my_block], device_id={"head": peer}, device_id_type=MESH,
        ).start()

    def post_all(src, dst, sem, recv, late=None):
        @pl.loop(1, zs)
        def _(i):
            peer_z = chip_at(zs - i)

            def both():
                post(src, dst, sem, recv, 2 * peer_z + core)
                post(src, dst, sem, recv, 2 * peer_z + 1 - core)

            if late is None:
                both()
            else:
                pl.when(lax.div(peer_z, zs // 2) == late)(both)

    with jax.named_scope("post"):
        post_all(k_send, k_all, 0, k_sem)
        post(k_send, k_all, 0, k_sem, 2 * z + 1 - core)

    with jax.named_scope("errors"):
        load_v.wait()
        load_g.wait()
        load_s.wait()

        @pl.loop(0, blocks)
        def _(b):
            at = block_rows(b)
            errors[b] = jnp.where(causal, dot(g_all[at], v_all[at], 1, 1), 0.0).astype(BF16)

    def wait_k(b):
        pltpu.make_async_copy(
            k_all.at[pl.ds(b * SPAN, SPAN)], k_all.at[pl.ds(b * SPAN, SPAN)], k_sem.at[b]
        ).wait()

    with jax.named_scope("kwait"):
        for b in range(blocks):
            wait_k(b)

    quarter = dim // XS
    far_y = sorted(range(1, ys), key=lambda i: -min(i, ys - i))

    def send_x(which, src_of, dst, i):
        to = lax.rem(x + i, XS)
        pltpu.make_async_remote_copy(
            src_ref=src_of(to), dst_ref=dst, send_sem=ex_send.at[which],
            recv_sem=ex_recv.at[which], device_id={"ctx": y * XS + to}, device_id_type=MESH,
        ).start()

    def stage_quarters(n, total):
        own_quarter[n] = total.reshape(XS, quarter, dim)
        for i in FAR_X:
            send_x(3 * n, lambda to: own_quarter.at[n, to], row_in.at[n, x], i)
        row_in[n, x] = own_quarter[n, x]

    def stage_rows(n):
        three = row_in.at[n, pl.ds(0, XS - 1)]
        pltpu.make_async_copy(three, three, ex_recv.at[3 * n]).wait()
        total = row_in[n, 0]
        for i in range(1, XS):
            total = total + row_in[n, i]
        row_sum[n] = total
        for i in far_y:
            pltpu.make_async_remote_copy(
                src_ref=row_sum.at[n], dst_ref=col_in.at[n, y], send_sem=ex_send.at[3 * n + 1],
                recv_sem=ex_recv.at[3 * n + 1],
                device_id={"ctx": lax.rem(y + i, ys) * XS + x}, device_id_type=MESH,
            ).start()
        col_in[n, y] = total

    def stage_back(n):
        rest = col_in.at[n, pl.ds(0, ys - 1)]
        pltpu.make_async_copy(rest, rest, ex_recv.at[3 * n + 1]).wait()
        zero = jnp.zeros((quarter, dim), F32)
        part = zero
        for i in range(ys):
            keep = (i > y) if n else (i < y)
            part = part + jnp.where(keep, col_in[n, i], zero)
        if n:
            grand = col_in[n, 0]
            for i in range(1, ys):
                grand = grand + col_in[n, i]
        members = range(XS - 1, -1, -1) if n else range(XS)
        for m in members:
            back_out[n, m, 0] = part
            if n:
                back_out[n, m, 1] = grand
            part = part + row_in[n, m]
        planes = 2 if n else 1
        for i in FAR_X:
            send_x(
                3 * n + 2, lambda to: back_out.at[n, to, pl.ds(0, planes)],
                back_in.at[n, x, pl.ds(0, planes)], i,
            )
        back_in[n, x, 0] = back_out[n, x, 0]
        if n:
            back_in[n, x, 1] = back_out[n, x, 1]

    def stage_done(n):
        planes = 2 if n else 1
        three = back_in.at[n, pl.ds(0, XS - 1), pl.ds(0, planes)]
        pltpu.make_async_copy(three, three, ex_recv.at[3 * n + 2]).wait()

    total = jnp.zeros((dim, dim), F32)
    for b in range(blocks):
        at = pl.ds(b * SPAN, SPAN)
        kv_blk[b] = total
        total = total + dot(k_all[at], v_all[at], 0, 0)
    with jax.named_scope("kvq"):
        stage_quarters(0, total)

    with jax.named_scope("postq"):
        post_all(q_send, q_all, 1, q_sem, 0)
        post_all(q_send, q_all, 1, q_sem, 1)
        post(q_send, q_all, 1, q_sem, 2 * z + 1 - core)

    def inner_query_grad(b):
        at = block_rows(b)
        qgrad_part[at] = dot(errors[b], k_all[at], 1, 0)

    with jax.named_scope("iqg01"):
        inner_query_grad(0)
        inner_query_grad(1)
    with jax.named_scope("rows0"):
        stage_rows(0)
    with jax.named_scope("iqg23"):
        inner_query_grad(2)
        inner_query_grad(3)
    with jax.named_scope("back0"):
        stage_back(0)
    with jax.named_scope("done0"):
        stage_done(0)
    state_in = s_own[0] + back_in[0, :, 0].reshape(dim, dim)
    for b in range(blocks):
        kv_blk[b] = kv_blk[b] + state_in

    def attend(b):
        at = block_rows(b)
        with jax.named_scope("qwait"):
            pltpu.make_async_copy(q_all.at[at], q_all.at[at], q_sem.at[b]).wait()
        with jax.named_scope("attend"):
            q_b = q_all[at]
            low = jnp.where(causal, dot(q_b, k_all[at], 1, 1), 0.0).astype(BF16)
            scores[b] = low
            out = dot(q_b, kv_blk[b].astype(BF16), 1, 0) + dot(low, v_all[at], 1, 0)
            att_send[at] = (scale * out).astype(BF16)

    def give_back(owner):
        pltpu.make_async_remote_copy(
            src_ref=att_send.at[pl.ds(pl.multiple_of(owner * rows, rows), rows)],
            dst_ref=att_recv.at[me], send_sem=send_sem.at[2], recv_sem=att_sem,
            device_id={"head": owner}, device_id_type=MESH,
        ).start()

    def state_of_queries(b):
        at = block_rows(b)
        with jax.named_scope("qg"):
            qg_blk[b] = dot(q_all[at], g_all[at], 0, 0)

    @pl.loop(0, blocks)
    def _(i):
        b = i
        attend(b)

        @pl.loop(0, per_block)
        def _(j):
            owner = b * per_block + j

            @pl.when(owner != me)
            def _():
                give_back(owner)

        state_of_queries(b)

    pltpu.make_async_copy(att_send.at[my_rows], att_recv.at[me], att_sem).start()

    total = jnp.zeros((dim, dim), F32)
    for b in range(blocks - 1, -1, -1):
        own = qg_blk[b]
        qg_blk[b] = total
        total = total + own
    with jax.named_scope("qgq"):
        stage_quarters(1, total)

    def inner_grads(b):
        at = block_rows(b)
        kgrad_part[at] = dot(errors[b], q_all[at], 0, 0)
        vgrad_part[at] = dot(scores[b], g_all[at], 0, 0)

    def query_grad(b):
        at = block_rows(b)
        out = dot(g_all[at], kv_blk[b].astype(BF16), 1, 1) + qgrad_part[at]
        qgrad_out[at] = (scale * out).astype(BF16)

    with jax.named_scope("ig01"):
        inner_grads(0)
        inner_grads(1)
    with jax.named_scope("rows1"):
        stage_rows(1)
    with jax.named_scope("ig23"):
        inner_grads(2)
        inner_grads(3)
    with jax.named_scope("qgrad"):
        for b in range(blocks):
            query_grad(b)
    with jax.named_scope("back1"):
        stage_back(1)
    with jax.named_scope("done1"):
        stage_done(1)
    after = back_in[1, :, 0].reshape(dim, dim)
    sgrad_out[0] = scale * back_in[1, :, 1].reshape(dim, dim)
    for b in range(blocks):
        at = pl.ds(b * SPAN, SPAN)
        low = (after + qg_blk[b]).astype(BF16)
        kgrad_out[at] = (scale * (dot(v_all[at], low, 1, 1) + kgrad_part[at])).astype(BF16)
        vgrad_out[at] = (scale * (dot(k_all[at], low, 1, 0) + vgrad_part[at])).astype(BF16)

    with jax.named_scope("attwait"):
        pltpu.make_async_copy(att_recv, att_recv, att_sem).wait()
    for h in range(heads):
        att_out[:, h * dim : (h + 1) * dim] = att_recv[h]

    others = pl.ds(0, heads - 1)
    pltpu.make_async_copy(k_send.at[others], k_send.at[others], send_sem.at[0]).wait()
    pltpu.make_async_copy(q_send.at[others], q_send.at[others], send_sem.at[1]).wait()
    pltpu.make_async_copy(att_recv.at[others], att_recv.at[others], send_sem.at[2]).wait()
    for n in range(2):
        three = row_in.at[n, pl.ds(0, XS - 1)]
        pltpu.make_async_copy(three, three, ex_send.at[3 * n]).wait()
        rest = col_in.at[n, pl.ds(0, ys - 1)]
        pltpu.make_async_copy(rest, rest, ex_send.at[3 * n + 1]).wait()
        three = back_in.at[n, pl.ds(0, XS - 1), pl.ds(0, 2 if n else 1)]
        pltpu.make_async_copy(three, three, ex_send.at[3 * n + 2]).wait()


def write_out(*refs):
    sem = refs[-1]
    copies = [pltpu.make_async_copy(refs[i], refs[5 + i], sem.at[i]) for i in range(5)]
    for copy in copies:
        copy.start()
    for copy in copies:
        copy.wait()


def local(zs, ys, query_rows, key_rows, value_rows, out_grad, entry_state):
    rows, features = query_rows.shape
    length, dim = value_rows.shape
    heads = 2 * zs
    blocks = length // SPAN
    scale = 1.0 / math.sqrt(dim * length * ys * XS)
    quarter = dim // XS
    any_spec = pl.BlockSpec(memory_space=pl.ANY)
    hbm_spec = pl.BlockSpec(memory_space=pltpu.HBM)
    vmem_spec = pl.BlockSpec(memory_space=pltpu.VMEM)
    dma = pltpu.SemaphoreType.DMA
    wide = (length, dim)
    results = pl.pallas_call(
        functools.partial(kernel, (zs, ys, rows, dim, blocks, scale)),
        out_shape=(
            jax.ShapeDtypeStruct((rows, features), BF16),
            jax.ShapeDtypeStruct(wide, BF16),
            jax.ShapeDtypeStruct(wide, BF16),
            jax.ShapeDtypeStruct(wide, BF16),
            jax.ShapeDtypeStruct((1, dim, dim), F32),
        ),
        in_specs=[hbm_spec] * 5,
        out_specs=[vmem_spec] * 5,
        scratch_shapes=[
            pltpu.VMEM((heads, rows, dim), BF16),
            pltpu.VMEM((heads, rows, dim), BF16),
            pltpu.VMEM(wide, BF16),
            pltpu.VMEM(wide, BF16),
            pltpu.VMEM(wide, BF16),
            pltpu.VMEM(wide, BF16),
            pltpu.VMEM((1, dim, dim), F32),
            pltpu.VMEM(wide, BF16),
            pltpu.VMEM((heads, rows, dim), BF16),
            pltpu.VMEM((blocks, SPAN, SPAN), BF16),
            pltpu.VMEM((blocks, SPAN, SPAN), BF16),
            pltpu.VMEM((blocks, dim, dim), F32),
            pltpu.VMEM((blocks, dim, dim), F32),
            pltpu.VMEM(wide, F32),
            pltpu.VMEM(wide, F32),
            pltpu.VMEM(wide, F32),
            pltpu.VMEM((2, XS, quarter, dim), F32),
            pltpu.VMEM((2, XS, quarter, dim), F32),
            pltpu.VMEM((2, quarter, dim), F32),
            pltpu.VMEM((2, ys, quarter, dim), F32),
            pltpu.VMEM((2, XS, 2, quarter, dim), F32),
            pltpu.VMEM((2, XS, 2, quarter, dim), F32),
            dma((5,)),
            dma((3,)),
            dma((blocks,)),
            dma((blocks,)),
            dma,
            dma((6,)),
            dma((6,)),
        ],
        compiler_params=pltpu.CompilerParams(
            collective_id=0, has_side_effects=True, vmem_limit_bytes=40 * 1024 * 1024
        ),
        name="layer",
    )(*(pltpu.with_memory_space_constraint(a, pltpu.HBM) for a in (query_rows, key_rows, value_rows, out_grad, entry_state)))
    return pl.pallas_call(
        write_out,
        out_shape=tuple(jax.ShapeDtypeStruct(r.shape, r.dtype) for r in results),
        in_specs=[vmem_spec] * 5,
        out_specs=[hbm_spec] * 5,
        scratch_shapes=[dma((5,))],
        compiler_params=pltpu.CompilerParams(vmem_limit_bytes=16 * 1024 * 1024),
        name="write_out",
    )(*results)


def solution(mesh):
    ys = mesh.shape["ctx"] // XS
    zs = mesh.shape["head"] // 2
    tokens = P(("ctx", "head"), None)
    split = P("ctx", "head")
    state = P("head", None, None)
    return jax.shard_map(
        functools.partial(local, zs, ys),
        mesh=mesh,
        in_specs=(tokens, tokens, split, split, state),
        out_specs=(tokens, split, split, split, state),
        check_vma=False,
    )
```

```python
import functools
import math

import jax
import jax.numpy as jnp
from jax import lax
from jax.experimental import pallas as pl
from jax.experimental.pallas import tpu as pltpu
from jax.sharding import PartitionSpec as P

SPAN = 384
XS = 4
FAR_X = (2, 1, 3)
MESH = pl.DeviceIdType.MESH
F32 = jnp.float32
BF16 = jnp.bfloat16


def dot(a, b, ca, cb):
    return lax.dot_general(a, b, (((ca,), (cb,)), ((), ())), preferred_element_type=F32)


def kernel(
    cfg,
    q_hbm, k_hbm, v_hbm, g_hbm, s_hbm,
    att_out, qgrad_out, kgrad_out, vgrad_out, sgrad_out,
    k_send, q_send, k_all, q_all, v_all, g_all, s_own,
    att_send, att_recv,
    errors, scores, kv_blk, qg_blk, qgrad_part, kgrad_part, vgrad_part,
    own_quarter, row_in, row_sum, col_in, back_out, back_in,
    load_sem, send_sem, k_sem, q_sem, att_sem,
    ex_send, ex_recv,
):
    zs, ys, rows, dim, blocks, scale = cfg
    heads = 2 * zs
    per_block = SPAN // rows
    ctx = lax.axis_index("ctx")
    me = lax.axis_index("head")
    z = lax.div(me, 2)
    core = lax.rem(me, 2)
    y = lax.div(ctx, XS)
    x = lax.rem(ctx, XS)
    my_block = lax.div(me, per_block)
    my_rows = pl.ds(pl.multiple_of(me * rows, rows), rows)

    def columns(h):
        return pl.ds(pl.multiple_of(h * dim, dim), dim)

    def block_rows(b):
        return pl.ds(pl.multiple_of(b * SPAN, SPAN), SPAN)

    barrier = pltpu.get_barrier_semaphore()

    def greet(where):
        pl.semaphore_signal(barrier, inc=1, device_id=where, device_id_type=MESH)

    def chip_at(i):
        step = lax.div(i + 1, 2) * (2 * lax.rem(i, 2) - 1)
        return lax.rem(z + step + zs, zs)

    @pl.loop(1, zs)
    def _(i):
        far = chip_at(zs - i)
        greet({"head": 2 * far})
        greet({"head": 2 * far + 1})

    greet({"head": 2 * z + 1 - core})

    @pl.loop(1, XS)
    def _(i):
        greet({"ctx": y * XS + lax.rem(x + i, XS)})

    @pl.loop(1, ys)
    def _(i):
        greet({"ctx": lax.rem(y + i, ys) * XS + x})

    def load_pieces(src, dst, sem):
        @pl.loop(0, heads)
        def _(h):
            pltpu.make_async_copy(src.at[:, columns(h)], dst.at[h], load_sem.at[sem]).start()

    load_v = pltpu.make_async_copy(v_hbm, v_all, load_sem.at[2])
    load_g = pltpu.make_async_copy(g_hbm, g_all, load_sem.at[3])
    load_s = pltpu.make_async_copy(s_hbm, s_own, load_sem.at[4])
    with jax.named_scope("loads"):
        load_v.start()
        load_g.start()
        load_pieces(k_hbm, k_send, 0)
        pltpu.make_async_copy(k_hbm.at[:, columns(me)], k_all.at[my_rows], k_sem.at[my_block]).start()
        load_pieces(q_hbm, q_send, 1)
        pltpu.make_async_copy(q_hbm.at[:, columns(me)], q_all.at[my_rows], q_sem.at[my_block]).start()
        load_s.start()

    causal = lax.broadcasted_iota(jnp.int32, (SPAN, SPAN), 0) >= lax.broadcasted_iota(
        jnp.int32, (SPAN, SPAN), 1
    )

    with jax.named_scope("loadwait"):
        pltpu.make_async_copy(k_send, k_send, load_sem.at[0]).wait()
        pltpu.make_async_copy(q_send, q_send, load_sem.at[1]).wait()
    with jax.named_scope("barrier"):
        pl.semaphore_wait(barrier, heads - 1 + XS - 1 + ys - 1)

    def post(src, dst, sem, recv, peer):
        pltpu.make_async_remote_copy(
            src_ref=src.at[peer], dst_ref=dst.at[my_rows], send_sem=send_sem.at[sem],
            recv_sem=recv.at[my_block], device_id={"head": peer}, device_id_type=MESH,
        ).start()

    def post_all(src, dst, sem, recv, late=None):
        @pl.loop(1, zs)
        def _(i):
            peer_z = chip_at(zs - i)

            def both():
                post(src, dst, sem, recv, 2 * peer_z + core)
                post(src, dst, sem, recv, 2 * peer_z + 1 - core)

            if late is None:
                both()
            else:
                pl.when(lax.div(peer_z, zs // 2) == late)(both)

    with jax.named_scope("post"):
        post_all(k_send, k_all, 0, k_sem)
        post(k_send, k_all, 0, k_sem, 2 * z + 1 - core)

    with jax.named_scope("errors"):
        load_v.wait()
        load_g.wait()
        load_s.wait()

        @pl.loop(0, blocks)
        def _(b):
            at = block_rows(b)
            errors[b] = jnp.where(causal, dot(g_all[at], v_all[at], 1, 1), 0.0).astype(BF16)

    def wait_k(b):
        pltpu.make_async_copy(
            k_all.at[block_rows(b)], k_all.at[block_rows(b)], k_sem.at[b]
        ).wait()

    my_half = lax.div(z, zs // 2)

    def wait_half(h):
        @pl.loop(0, blocks // 2)
        def _(i):
            wait_k(h * (blocks // 2) + i)

    with jax.named_scope("kwait"):
        wait_half(my_half)
    with jax.named_scope("postq"):
        post_all(q_send, q_all, 1, q_sem, 0)
    with jax.named_scope("kwait"):
        wait_half(1 - my_half)

    quarter = dim // XS
    far_y = sorted(range(1, ys), key=lambda i: -min(i, ys - i))

    def send_x(which, src_of, dst, i):
        to = lax.rem(x + i, XS)
        pltpu.make_async_remote_copy(
            src_ref=src_of(to), dst_ref=dst, send_sem=ex_send.at[which],
            recv_sem=ex_recv.at[which], device_id={"ctx": y * XS + to}, device_id_type=MESH,
        ).start()

    def stage_quarters(n, total):
        own_quarter[n] = total.reshape(XS, quarter, dim)
        for i in FAR_X:
            send_x(3 * n, lambda to: own_quarter.at[n, to], row_in.at[n, x], i)
        row_in[n, x] = own_quarter[n, x]

    def stage_rows(n):
        three = row_in.at[n, pl.ds(0, XS - 1)]
        pltpu.make_async_copy(three, three, ex_recv.at[3 * n]).wait()
        total = row_in[n, 0]
        for i in range(1, XS):
            total = total + row_in[n, i]
        row_sum[n] = total
        for i in far_y:
            pltpu.make_async_remote_copy(
                src_ref=row_sum.at[n], dst_ref=col_in.at[n, y], send_sem=ex_send.at[3 * n + 1],
                recv_sem=ex_recv.at[3 * n + 1],
                device_id={"ctx": lax.rem(y + i, ys) * XS + x}, device_id_type=MESH,
            ).start()
        col_in[n, y] = total

    def stage_back(n):
        rest = col_in.at[n, pl.ds(0, ys - 1)]
        pltpu.make_async_copy(rest, rest, ex_recv.at[3 * n + 1]).wait()
        zero = jnp.zeros((quarter, dim), F32)
        part = zero
        for i in range(ys):
            keep = (i > y) if n else (i < y)
            part = part + jnp.where(keep, col_in[n, i], zero)
        if n:
            grand = col_in[n, 0]
            for i in range(1, ys):
                grand = grand + col_in[n, i]
        members = range(XS - 1, -1, -1) if n else range(XS)
        for m in members:
            back_out[n, m, 0] = part
            if n:
                back_out[n, m, 1] = grand
            part = part + row_in[n, m]
        planes = 2 if n else 1
        for i in FAR_X:
            send_x(
                3 * n + 2, lambda to: back_out.at[n, to, pl.ds(0, planes)],
                back_in.at[n, x, pl.ds(0, planes)], i,
            )
        back_in[n, x, 0] = back_out[n, x, 0]
        if n:
            back_in[n, x, 1] = back_out[n, x, 1]

    def stage_done(n):
        planes = 2 if n else 1
        three = back_in.at[n, pl.ds(0, XS - 1), pl.ds(0, planes)]
        pltpu.make_async_copy(three, three, ex_recv.at[3 * n + 2]).wait()

    total = jnp.zeros((dim, dim), F32)
    for b in range(blocks):
        at = pl.ds(b * SPAN, SPAN)
        kv_blk[b] = total
        total = total + dot(k_all[at], v_all[at], 0, 0)
    with jax.named_scope("kvq"):
        stage_quarters(0, total)

    with jax.named_scope("postq"):
        post_all(q_send, q_all, 1, q_sem, 1)
        post(q_send, q_all, 1, q_sem, 2 * z + 1 - core)

    def inner_query_grad(b):
        at = block_rows(b)
        qgrad_part[at] = dot(errors[b], k_all[at], 1, 0)

    with jax.named_scope("iqg01"):
        inner_query_grad(0)
        inner_query_grad(1)
    with jax.named_scope("rows0"):
        stage_rows(0)
    with jax.named_scope("iqg23"):
        inner_query_grad(2)
        inner_query_grad(3)
    with jax.named_scope("back0"):
        stage_back(0)
    with jax.named_scope("done0"):
        stage_done(0)
    state_in = s_own[0] + back_in[0, :, 0].reshape(dim, dim)
    for b in range(blocks):
        kv_blk[b] = kv_blk[b] + state_in

    def attend(b):
        at = block_rows(b)
        with jax.named_scope("qwait"):
            pltpu.make_async_copy(q_all.at[at], q_all.at[at], q_sem.at[b]).wait()
        with jax.named_scope("attend"):
            q_b = q_all[at]
            low = jnp.where(causal, dot(q_b, k_all[at], 1, 1), 0.0).astype(BF16)
            scores[b] = low
            out = dot(q_b, kv_blk[b].astype(BF16), 1, 0) + dot(low, v_all[at], 1, 0)
            att_send[at] = (scale * out).astype(BF16)

    def give_back(owner):
        pltpu.make_async_remote_copy(
            src_ref=att_send.at[pl.ds(pl.multiple_of(owner * rows, rows), rows)],
            dst_ref=att_recv.at[me], send_sem=send_sem.at[2], recv_sem=att_sem,
            device_id={"head": owner}, device_id_type=MESH,
        ).start()

    def state_of_queries(b):
        at = block_rows(b)
        with jax.named_scope("qg"):
            qg_blk[b] = dot(q_all[at], g_all[at], 0, 0)

    @pl.loop(0, blocks)
    def _(i):
        b = i
        attend(b)

        @pl.loop(0, per_block)
        def _(j):
            owner = b * per_block + j

            @pl.when(owner != me)
            def _():
                give_back(owner)

        state_of_queries(b)

    pltpu.make_async_copy(att_send.at[my_rows], att_recv.at[me], att_sem).start()

    total = jnp.zeros((dim, dim), F32)
    for b in range(blocks - 1, -1, -1):
        own = qg_blk[b]
        qg_blk[b] = total
        total = total + own
    with jax.named_scope("qgq"):
        stage_quarters(1, total)

    def inner_grads(b):
        at = block_rows(b)
        kgrad_part[at] = dot(errors[b], q_all[at], 0, 0)
        vgrad_part[at] = dot(scores[b], g_all[at], 0, 0)

    def query_grad(b):
        at = block_rows(b)
        out = dot(g_all[at], kv_blk[b].astype(BF16), 1, 1) + qgrad_part[at]
        qgrad_out[at] = (scale * out).astype(BF16)

    with jax.named_scope("ig01"):
        inner_grads(0)
        inner_grads(1)
    with jax.named_scope("rows1"):
        stage_rows(1)
    with jax.named_scope("ig23"):
        inner_grads(2)
        inner_grads(3)
    with jax.named_scope("qgrad"):
        for b in range(blocks):
            query_grad(b)
    with jax.named_scope("back1"):
        stage_back(1)
    with jax.named_scope("done1"):
        stage_done(1)
    after = back_in[1, :, 0].reshape(dim, dim)
    sgrad_out[0] = scale * back_in[1, :, 1].reshape(dim, dim)
    for b in range(blocks):
        at = pl.ds(b * SPAN, SPAN)
        low = (after + qg_blk[b]).astype(BF16)
        kgrad_out[at] = (scale * (dot(v_all[at], low, 1, 1) + kgrad_part[at])).astype(BF16)
        vgrad_out[at] = (scale * (dot(k_all[at], low, 1, 0) + vgrad_part[at])).astype(BF16)

    with jax.named_scope("attwait"):
        pltpu.make_async_copy(att_recv, att_recv, att_sem).wait()
    for h in range(heads):
        att_out[:, h * dim : (h + 1) * dim] = att_recv[h]

    others = pl.ds(0, heads - 1)
    pltpu.make_async_copy(k_send.at[others], k_send.at[others], send_sem.at[0]).wait()
    pltpu.make_async_copy(q_send.at[others], q_send.at[others], send_sem.at[1]).wait()
    pltpu.make_async_copy(att_recv.at[others], att_recv.at[others], send_sem.at[2]).wait()
    for n in range(2):
        three = row_in.at[n, pl.ds(0, XS - 1)]
        pltpu.make_async_copy(three, three, ex_send.at[3 * n]).wait()
        rest = col_in.at[n, pl.ds(0, ys - 1)]
        pltpu.make_async_copy(rest, rest, ex_send.at[3 * n + 1]).wait()
        three = back_in.at[n, pl.ds(0, XS - 1), pl.ds(0, 2 if n else 1)]
        pltpu.make_async_copy(three, three, ex_send.at[3 * n + 2]).wait()


def write_out(*refs):
    sem = refs[-1]
    copies = [pltpu.make_async_copy(refs[i], refs[5 + i], sem.at[i]) for i in range(5)]
    for copy in copies:
        copy.start()
    for copy in copies:
        copy.wait()


def local(zs, ys, query_rows, key_rows, value_rows, out_grad, entry_state):
    rows, features = query_rows.shape
    length, dim = value_rows.shape
    heads = 2 * zs
    blocks = length // SPAN
    scale = 1.0 / math.sqrt(dim * length * ys * XS)
    quarter = dim // XS
    any_spec = pl.BlockSpec(memory_space=pl.ANY)
    hbm_spec = pl.BlockSpec(memory_space=pltpu.HBM)
    vmem_spec = pl.BlockSpec(memory_space=pltpu.VMEM)
    dma = pltpu.SemaphoreType.DMA
    wide = (length, dim)
    results = pl.pallas_call(
        functools.partial(kernel, (zs, ys, rows, dim, blocks, scale)),
        out_shape=(
            jax.ShapeDtypeStruct((rows, features), BF16),
            jax.ShapeDtypeStruct(wide, BF16),
            jax.ShapeDtypeStruct(wide, BF16),
            jax.ShapeDtypeStruct(wide, BF16),
            jax.ShapeDtypeStruct((1, dim, dim), F32),
        ),
        in_specs=[hbm_spec] * 5,
        out_specs=[vmem_spec] * 5,
        scratch_shapes=[
            pltpu.VMEM((heads, rows, dim), BF16),
            pltpu.VMEM((heads, rows, dim), BF16),
            pltpu.VMEM(wide, BF16),
            pltpu.VMEM(wide, BF16),
            pltpu.VMEM(wide, BF16),
            pltpu.VMEM(wide, BF16),
            pltpu.VMEM((1, dim, dim), F32),
            pltpu.VMEM(wide, BF16),
            pltpu.VMEM((heads, rows, dim), BF16),
            pltpu.VMEM((blocks, SPAN, SPAN), BF16),
            pltpu.VMEM((blocks, SPAN, SPAN), BF16),
            pltpu.VMEM((blocks, dim, dim), F32),
            pltpu.VMEM((blocks, dim, dim), F32),
            pltpu.VMEM(wide, F32),
            pltpu.VMEM(wide, F32),
            pltpu.VMEM(wide, F32),
            pltpu.VMEM((2, XS, quarter, dim), F32),
            pltpu.VMEM((2, XS, quarter, dim), F32),
            pltpu.VMEM((2, quarter, dim), F32),
            pltpu.VMEM((2, ys, quarter, dim), F32),
            pltpu.VMEM((2, XS, 2, quarter, dim), F32),
            pltpu.VMEM((2, XS, 2, quarter, dim), F32),
            dma((5,)),
            dma((3,)),
            dma((blocks,)),
            dma((blocks,)),
            dma,
            dma((6,)),
            dma((6,)),
        ],
        compiler_params=pltpu.CompilerParams(
            collective_id=0, has_side_effects=True, vmem_limit_bytes=40 * 1024 * 1024
        ),
        name="layer",
    )(*(pltpu.with_memory_space_constraint(a, pltpu.HBM) for a in (query_rows, key_rows, value_rows, out_grad, entry_state)))
    return pl.pallas_call(
        write_out,
        out_shape=tuple(jax.ShapeDtypeStruct(r.shape, r.dtype) for r in results),
        in_specs=[vmem_spec] * 5,
        out_specs=[hbm_spec] * 5,
        scratch_shapes=[dma((5,))],
        compiler_params=pltpu.CompilerParams(vmem_limit_bytes=16 * 1024 * 1024),
        name="write_out",
    )(*results)


def solution(mesh):
    ys = mesh.shape["ctx"] // XS
    zs = mesh.shape["head"] // 2
    tokens = P(("ctx", "head"), None)
    split = P("ctx", "head")
    state = P("head", None, None)
    return jax.shard_map(
        functools.partial(local, zs, ys),
        mesh=mesh,
        in_specs=(tokens, tokens, split, split, state),
        out_specs=(tokens, split, split, split, state),
        check_vma=False,
    )
```
